32 devices in a mesh: groups: 2 (over y), tile: 8 (over z, x), band: 2 (over core).
Axes of the slice: x: 2, y: 2, z: 4, core: 2. Of those that a mesh axis runs over, the one named last changes fastest.
Arguments:
- cube: bfloat16 [128, 128, 1024], P(('groups', 'band'), None, 'tile'), parts along dimension 0, may hold values from -6 to 6
- kernels: bfloat16 [32, 64, 192], replicated, may hold values from -0.0546875 to 0.0546875
- zone_map: int32 [16, 128], P(None, 'tile'), may hold values from 0 to 3
- kernel_index: int32 [64, 4], replicated, may hold values from 0 to 31
- measurement: float32 [256, 1024], P(('groups', 'tile', 'band')), parts along dimension 0, may hold values from -6 to 6
- step_size: float32 [64], P('band'), may hold values from 1 to 4
- spectral_weight: float32 [64], P('band'), may hold values from 0.05 to 0.3
- prior_taps: float32 [3, 3], replicated, may hold values from -0.6 to 0.6
Outputs:
- updated: bfloat16 [128, 128, 1024], P(('groups', 'band'), None, 'tile'), parts along dimension 0
- residual: float32 [256, 1024], P(('groups', 'tile', 'band')), parts along dimension 0
The draws below stay inside these ranges and needn't reach their ends.
There are 2 independent parts, one for each index of `groups`. The reference program is written for one: setup_inputs(seed, part) draws one part's arguments, and reference() takes and returns one part's arrays. A program takes and returns all parts, laid end to end along the dimension named above; an argument that names none is the same for every part. Nothing has to cross between parts.
Inputs may be any that keep to these rules, and one draw needn't show every extreme that they name: `kernel_index`: row of the kernel table.
All inputs are finite; a program needn't handle non-finite values.
Results may differ from the reference program's by a relative error of at most 0.0031.
Values may be sent and summed in bfloat16 or wider, within the bound.
A program may use at most 128 MiB of HBM per device.

```python
import math
import jax
import jax.numpy as jnp
from jax import lax

BLOCK = 8
SUP = 3
ZONES = 4
NK = 32
BANDS = 64
H = 128
WT = 128
W = 1024
N_TILE = 8


def touch_ends(array, rng, low, largest):
    dims = array.shape
    spot = [jax.random.randint(jax.random.fold_in(rng, axis), (), 0, dims[axis]) for axis in range(len(dims))]
    array = array.at[tuple(spot)].set(low)
    longest = dims.index(max(dims))
    spot[longest] = (spot[longest] + 1) % dims[longest]
    return array.at[tuple(spot)].set(largest)


def steps_of(key, shape, split, least, top_value):
    gain = 1.0
    for axis_at, shards_of in split:
        draws = jax.random.uniform(jax.random.fold_in(jax.random.fold_in(key, 6), axis_at), (shards_of,), jnp.float32, least / len(split), top_value / len(split))
        gain = gain * jnp.repeat(jnp.exp(draws), shape[axis_at] // shards_of).reshape((-1,) + (1,) * (len(shape) - 1 - axis_at))
    return gain


def centred(rng, shape, width, limit, cuts=(), kind=jnp.bfloat16):
    factor_of = steps_of(rng, shape, cuts, -0.22, 0.18) if cuts else 1.0
    entries = jax.random.normal(rng, shape, jnp.float32) * width * factor_of
    return jnp.minimum(jnp.maximum(entries, -limit), limit).astype(kind)


def setup_inputs(seed: int = 0, part: int = 0) -> dict:
    key_list = jax.random.split(jax.random.key(seed), 9)
    part_keys = jax.random.split(jax.random.fold_in(key_list[8], part), 9)
    cube = centred(part_keys[0], (BANDS, H, W), 1.0, 6.0, ((0, 2), (2, 8)))
    kernels = centred(key_list[1], (NK, BLOCK * BLOCK, SUP * BLOCK * BLOCK), (BANDS * SUP * BLOCK * BLOCK) ** -0.5, 0.0546875)
    zone_map = touch_ends(jax.random.randint(key_list[2], (H // BLOCK, W // BLOCK), 0, ZONES), jax.random.fold_in(key_list[2], 1), 0, ZONES - 1).astype(jnp.int32)
    kernel_index = touch_ends(jax.random.randint(key_list[3], (BANDS, ZONES), 0, NK), jax.random.fold_in(key_list[3], 1), 0, NK - 1).astype(jnp.int32)
    measurement = centred(part_keys[4], (H, W), 1.0, 6.0, ((0, 16),), jnp.float32)
    step_size = jnp.clip(jnp.exp(math.log(4.0) - 1.3862944 * jax.random.uniform(key_list[5], (BANDS,), jnp.float32) ** steps_of(key_list[5], (BANDS,), ((0, 2),), -0.2, 0.2)), 1.0, 4.0)
    spectral_weight = jnp.clip(jnp.exp(math.log(0.3) - 1.7917595 * jax.random.uniform(key_list[6], (BANDS,), jnp.float32) ** steps_of(key_list[6], (BANDS,), ((0, 2),), -0.2, 0.2)), 0.05, 0.3)
    prior_taps = centred(key_list[7], (3, 3), 0.15, 0.6, (), jnp.float32)
    return {"cube": cube, "kernels": kernels, "zone_map": zone_map, "kernel_index": kernel_index, "measurement": measurement, "step_size": step_size, "spectral_weight": spectral_weight, "prior_taps": prior_taps}


def to_blocks(piece):
    bands, rows, cols = piece.shape
    grid = piece.reshape(bands, rows // BLOCK, BLOCK, cols // BLOCK, BLOCK)
    return grid.transpose(1, 3, 0, 2, 4).reshape((rows // BLOCK) * (cols // BLOCK), bands * BLOCK * BLOCK)


def from_blocks(flat, bands, rows, cols):
    grid = flat.reshape(rows // BLOCK, cols // BLOCK, bands, BLOCK, BLOCK)
    return grid.transpose(2, 0, 3, 1, 4).reshape(bands, rows, cols)


def spread_down(sensor_blocks, block_rows, block_cols):
    pixels = BLOCK * BLOCK
    half = SUP // 2
    offsets = sensor_blocks.reshape(block_rows, block_cols, SUP, pixels)
    padded = jnp.pad(offsets, ((half, half), (0, 0), (0, 0), (0, 0)))
    total = jnp.zeros((block_rows, block_cols, pixels), jnp.float32)
    for shift_row in range(SUP):
        start = 2 * half - shift_row
        total = total + padded[start:start + block_rows, :, shift_row]
    return total.reshape(block_rows * block_cols, pixels)


def gather_down(image_blocks, block_rows, block_cols):
    pixels = BLOCK * BLOCK
    half = SUP // 2
    grid = image_blocks.reshape(block_rows, block_cols, pixels)
    rim = jnp.pad(grid, ((half, half), (0, 0), (0, 0)))
    stacked = jnp.stack([rim[shift_row:shift_row + block_rows] for shift_row in range(SUP)], axis=2)
    return stacked.reshape(block_rows * block_cols, SUP * pixels)


def reference(cube, kernels, zone_map, kernel_index, measurement, step_size, spectral_weight, prior_taps):
    pixels = BLOCK * BLOCK
    spread = SUP * pixels
    block_rows = H // BLOCK
    block_cols = WT // BLOCK
    width_all = WT * N_TILE
    chosen = kernels.astype(jnp.float32)[kernel_index]
    tables = [chosen[:, zone_number].reshape(BANDS * pixels, spread) for zone_number in range(ZONES)]
    tile_ids = jnp.arange(N_TILE, dtype=jnp.int32)

    def zone_masks(tile_number):
        zones = lax.dynamic_slice_in_dim(zone_map, (tile_number * block_cols).astype(jnp.int32), block_cols, 1)
        flat = zones.reshape(-1)
        return [(flat == zone_number).astype(jnp.float32)[:, None] for zone_number in range(ZONES)]

    def forward_tile(tile_number):
        piece = lax.dynamic_slice_in_dim(cube, (tile_number * WT).astype(jnp.int32), WT, 2).astype(jnp.float32)
        blocks = to_blocks(piece)
        masks = zone_masks(tile_number)
        sensor_blocks = jnp.zeros((blocks.shape[0], spread), jnp.float32)
        for zone_number in range(ZONES):
            sensor_blocks = sensor_blocks + jnp.dot(blocks * masks[zone_number], tables[zone_number], precision=lax.Precision.HIGHEST, preferred_element_type=jnp.float32)
        summed = spread_down(sensor_blocks, block_rows, block_cols)
        return from_blocks(summed, 1, H, WT)[0]

    sensor = lax.map(forward_tile, tile_ids).transpose(1, 0, 2).reshape(H, width_all)
    residual = sensor - measurement
    residual_half = residual.astype(jnp.bfloat16)
    padded_cube = jnp.pad(cube, ((1, 1), (1, 1), (1, 1)))

    def update_tile(tile_number):
        start = (tile_number * WT).astype(jnp.int32)
        rows_here = lax.dynamic_slice_in_dim(residual_half, start, WT, 1).astype(jnp.float32)
        stacked = gather_down(to_blocks(rows_here[None]), block_rows, block_cols)
        masks = zone_masks(tile_number)
        gradient = jnp.zeros((stacked.shape[0], BANDS * pixels), jnp.float32)
        for zone_number in range(ZONES):
            term = lax.dot_general(stacked, tables[zone_number], (((1,), (1,)), ((), ())), precision=lax.Precision.HIGHEST, preferred_element_type=jnp.float32)
            gradient = gradient + term * masks[zone_number]
        gradient = from_blocks(gradient, BANDS, H, WT)
        extended = lax.dynamic_slice_in_dim(padded_cube, start, WT + 2, 2).astype(jnp.float32)
        centre = extended[1:-1, 1:-1, 1:-1]
        spatial = jnp.zeros_like(centre)
        for row_tap in range(3):
            for col_tap in range(3):
                spatial = spatial + prior_taps[row_tap, col_tap] * extended[1:-1, row_tap:row_tap + H, col_tap:col_tap + WT]
        spectral = 2.0 * centre - extended[:-2, 1:-1, 1:-1] - extended[2:, 1:-1, 1:-1]
        prior = spatial + spectral_weight[:, None, None] * spectral
        return (centre - step_size[:, None, None] * (gradient + prior)).astype(jnp.bfloat16)

    updated = lax.map(update_tile, tile_ids).transpose(1, 2, 0, 3).reshape(BANDS, H, width_all)
    return updated, residual
```

```python
import functools

import jax
import jax.numpy as jnp
from jax import lax
from jax.experimental import pallas as pl
from jax.experimental.pallas import tpu as pltpu
from jax.sharding import PartitionSpec as P

BLOCK = 8
SUP = 3
ZONES = 4
PIX = BLOCK * BLOCK
F32 = jnp.float32
BF16 = jnp.bfloat16
MESH = pl.DeviceIdType.MESH
NT = (((1,), (1,)), ((), ()))


def iota(shape, dim):
    return lax.broadcasted_iota(jnp.int32, shape, dim)


def onehot(mask):
    return jnp.where(mask, 1.0, 0.0).astype(BF16)


def dot(a, b):
    return jnp.dot(a, b, preferred_element_type=F32)


def dot_nt(a, b):
    return lax.dot_general(a, b, NT, preferred_element_type=F32)


def kernel(
    tiles,
    cube_ref, kern_ref, zone_ref, meas_ref, kidx_ref, step_ref, weight_ref, taps_ref,
    out_ref, res_ref,
    perm_ref, xcat_ref, at_ref, table_ref, kp_ref, grad_ref, prior_ref,
    edge_ref, hsend_ref, hrecv_ref, halo_ref, mine_ref, theirs_ref, rblk_ref,
    send_sem, recv_sem,
):
    bands = cube_ref.shape[0]
    rows = bands * BLOCK
    h = lax.axis_index("band")
    t = lax.axis_index("tile")
    group = lax.axis_index("groups")
    partner = (group, t, 1 - h)
    left = (group, lax.rem(t + tiles - 1, tiles), h)
    right = (group, lax.rem(t + 1, tiles), h)

    barrier = pltpu.get_barrier_semaphore()
    for device in (partner, left, right):
        pl.semaphore_signal(barrier, inc=1, device_id=device, device_id_type=MESH)

    for pair in range(8):
        two = cube_ref[:, pair * 16 : pair * 16 + 16, :].astype(F32)
        for k in range(2):
            i = pair * 2 + k
            xcat_ref[:, i * 128 : i * 128 + 128] = (
                two[:, k * 8 : k * 8 + 8].reshape(rows, 128).astype(BF16)
            )

    sel_row = iota((2048, 128), 0)
    sel_lane = iota((2048, 128), 1)
    wanted = (sel_lane // 2) * 128 + jnp.where(sel_lane % 2 == 0, 127, 0)
    hsend_ref[...] = dot(xcat_ref[...], onehot(sel_row == wanted)).astype(BF16)

    pl.semaphore_wait(barrier, 3)
    copies = [
        pltpu.make_async_remote_copy(
            src_ref=src, dst_ref=dst, send_sem=send_sem.at[k], recv_sem=recv_sem.at[k],
            device_id=device, device_id_type=MESH,
        )
        for k, (src, dst, device) in enumerate(
            (
                (cube_ref.at[(bands - 1) * (1 - h)], edge_ref, partner),
                (hsend_ref, hrecv_ref.at[0], right),
                (hsend_ref, hrecv_ref.at[1], left),
                (mine_ref, theirs_ref, partner),
            )
        )
    ]
    for copy in copies[:3]:
        copy.start()

    for p in range(8):
        n = iota((128, 1024), 0)
        k = iota((128, 1024), 1)
        perm_ref[p * 128 : p * 128 + 128, :] = onehot(k == (n // 16) * 128 + (n % 16) * 8 + p)

    for half in range(2):
        blocks = dot_nt(perm_ref[...], xcat_ref[:, half * 1024 : half * 1024 + 1024])
        for p in range(8):
            at_ref[half * 128 : half * 128 + 128, p * rows : p * rows + rows] = blocks[
                p * 128 : p * 128 + 128
            ].astype(BF16)

    i = iota((256, 256), 0)
    j = iota((256, 256), 1)
    swap = onehot(j == (i // 64) * 64 + (i % 8) * 8 + (i // 8) % 8)
    kp_ref[:, :, 128:256] = jnp.zeros((kp_ref.shape[0], PIX, 128), F32)
    for g in range(kp_ref.shape[0] // 4):
        four = kern_ref[g * 4 : g * 4 + 4].reshape(256, SUP * PIX)
        kp_ref[g * 4 : g * 4 + 4, :, 0 : SUP * PIX] = dot(swap, four).reshape(4, PIX, SUP * PIX)

    def gather(pair, carry):
        for z in range(ZONES):
            first = kp_ref[kidx_ref[h * bands + pair * 2, z]]
            second = kp_ref[kidx_ref[h * bands + pair * 2 + 1, z]]
            for p in range(8):
                chunk = jnp.concatenate(
                    [first[p * 8 : p * 8 + 8], second[p * 8 : p * 8 + 8]], axis=0
                )
                at = pl.multiple_of(p * rows + pair * 16, 16)
                table_ref[pl.ds(at, 16), z * 256 : z * 256 + 256] = chunk.astype(BF16)
        return carry

    lax.fori_loop(0, bands // 2, gather, 0)

    zone = zone_ref[...].astype(F32).astype(BF16)
    spread_col = dot(onehot(iota((256, 16), 0) // 16 == iota((256, 16), 1)), zone)
    keep = iota((256, 16), 0) % 16 == iota((256, 16), 1)
    zone_col = jnp.sum(jnp.where(keep, spread_col, 0.0), axis=1, keepdims=True)
    spread_row = dot(zone, onehot(iota((16, 256), 1) % 16 == iota((16, 256), 0)))
    keep = iota((16, 256), 1) // 16 == iota((16, 256), 0)
    zone_row = jnp.sum(jnp.where(keep, spread_row, 0.0), axis=0, keepdims=True)

    every = dot(at_ref[...], table_ref[...])
    chosen = jnp.zeros((256, 256), F32)
    for z in range(ZONES):
        chosen = jnp.where(zone_col == float(z), every[:, z * 256 : z * 256 + 256], chosen)
    across = chosen.T
    lane = iota((PIX, 256), 1)
    up = pltpu.roll(across[0:PIX], 240, 1)
    down = pltpu.roll(across[2 * PIX : 3 * PIX], 16, 1)
    partial = (
        across[PIX : 2 * PIX]
        + jnp.where(lane < 240, up, 0.0)
        + jnp.where(lane >= 16, down, 0.0)
    )
    for half in range(2):
        mine_ref[half * PIX : half * PIX + PIX, :] = partial[:, half * 128 : half * 128 + 128]
    copies[3].start()

    for copy in copies[:3]:
        copy.wait()
    even = iota((rows, 128), 1) % 2 == 0
    from_left = jnp.where(t > 0, hrecv_ref[0].astype(F32), 0.0)
    from_right = jnp.where(t < tiles - 1, hrecv_ref[1].astype(F32), 0.0)
    halo_ref[...] = jnp.where(even, from_left, from_right)

    lane = iota((128, 128), 1)
    row = iota((128, 128), 0)

    def prior_of(b, carry):
        x = cube_ref[b].astype(F32)
        edge = edge_ref[...].astype(F32)
        before = cube_ref[jnp.maximum(b - 1, 0)].astype(F32)
        after = cube_ref[jnp.minimum(b + 1, bands - 1)].astype(F32)
        before = jnp.where(b > 0, before, jnp.where(h > 0, edge, 0.0))
        after = jnp.where(b < bands - 1, after, jnp.where(h < 1, edge, 0.0))
        one = halo_ref[pl.ds(pl.multiple_of(b * 8, 8), 8), :]
        rim = jnp.concatenate(
            [pltpu.roll(one, 127 - 2 * i, 1) for i in range(16)], axis=0
        )
        west = pltpu.roll(jnp.where(lane == 127, rim, x), 1, 1)
        east = pltpu.roll(jnp.where(lane == 0, rim, x), 127, 1)
        terms = [
            taps_ref[a, 0] * west + taps_ref[a, 1] * x + taps_ref[a, 2] * east
            for a in range(3)
        ]
        spatial = (
            terms[1]
            + jnp.where(row > 0, pltpu.roll(terms[0], 1, 0), 0.0)
            + jnp.where(row < 127, pltpu.roll(terms[2], 127, 0), 0.0)
        )
        prior_ref[b] = spatial + weight_ref[b] * (2.0 * x - before - after)
        return carry

    lax.fori_loop(0, bands, prior_of, 0)

    copies[3].wait()
    mine_ref[...] = mine_ref[...] + theirs_ref[...]
    flat = jnp.concatenate(
        [
            jnp.concatenate(
                [
                    mine_ref[pl.ds(half * PIX + q, 8, stride=8), :]
                    for q in range(8)
                ],
                axis=1,
            )
            for half in range(2)
        ],
        axis=0,
    )
    high = flat.astype(BF16)
    rest = flat - high.astype(F32)
    mid = rest.astype(BF16)
    low = (rest - mid.astype(F32)).astype(BF16)
    parts = dot(jnp.concatenate([high, mid, low], axis=0), perm_ref[...])
    image = parts[0:16] + (parts[16:32] + parts[32:48])
    residual = []
    for i in range(16):
        half, k = i // 8, i % 8
        piece = (
            image[half * 8 : half * 8 + 8, k * 128 : k * 128 + 128]
            - meas_ref[i * 8 : i * 8 + 8, :]
        )
        res_ref[i * 8 : i * 8 + 8, :] = piece
        residual.append(piece)
    flat = jnp.concatenate(
        [jnp.concatenate(residual[half * 8 : half * 8 + 8], axis=1) for half in range(2)], axis=0
    ).astype(BF16)
    back = dot_nt(flat, perm_ref[...])
    for half in range(2):
        for q in range(8):
            rblk_ref[pl.ds(half * PIX + q, 8, stride=8), :] = back[
                half * 8 : half * 8 + 8, q * 128 : q * 128 + 128
            ]
    centre = jnp.concatenate([rblk_ref[0:PIX, :], rblk_ref[PIX : 2 * PIX, :]], axis=1)
    lane = iota((PIX, 256), 1)
    above = jnp.where(lane >= 16, pltpu.roll(centre, 16, 1), 0.0)
    below = jnp.where(lane < 240, pltpu.roll(centre, 240, 1), 0.0)
    stacked = jnp.concatenate([above, centre, below, jnp.zeros((PIX, 256), F32)], axis=0)
    zoned = jnp.concatenate(
        [jnp.where(zone_row == float(z), stacked, 0.0) for z in range(ZONES)], axis=0
    ).astype(BF16)

    for p in range(8):
        grad_ref[p] = dot(table_ref[p * rows : p * rows + rows, :], zoned)
    for half in range(2):
        wide = jnp.concatenate(
            [grad_ref[p, :, half * 128 : half * 128 + 128] for p in range(8)], axis=1
        )
        high = wide.astype(BF16)
        low = (wide - high.astype(F32)).astype(BF16)
        gradient = dot(high, perm_ref[...]) + dot(low, perm_ref[...])
        for k in range(8):
            i = half * 8 + k
            prior_ref[:, i * 8 : i * 8 + 8, :] = prior_ref[:, i * 8 : i * 8 + 8, :] + gradient[
                :, k * 128 : k * 128 + 128
            ].reshape(bands, 8, 128)

    def update(b, carry):
        out_ref[b] = (cube_ref[b].astype(F32) - step_ref[b] * prior_ref[b]).astype(BF16)
        return carry

    lax.fori_loop(0, bands, update, 0)


def per_device(
    tiles, cube, kernels, zone_map, kernel_index, measurement, step_size, spectral_weight,
    prior_taps,
):
    bands, height, width = cube.shape
    strip = measurement.shape[0]
    rows = bands * BLOCK
    moved = lax.all_to_all(measurement, "tile", split_axis=1, concat_axis=0, tiled=True)
    both = lax.all_gather(moved, "band", axis=0, tiled=False)
    image = both.reshape(2, tiles, strip, width).transpose(1, 0, 2, 3).reshape(height, width)
    vmem = pl.BlockSpec(memory_space=pltpu.VMEM)
    smem = pl.BlockSpec(memory_space=pltpu.SMEM)
    updated, residual = pl.pallas_call(
        functools.partial(kernel, tiles),
        out_shape=(
            jax.ShapeDtypeStruct(cube.shape, BF16),
            jax.ShapeDtypeStruct((height, width), F32),
        ),
        in_specs=[vmem] * 4 + [smem] * 4,
        out_specs=(vmem, vmem),
        scratch_shapes=[
            pltpu.VMEM((1024, 1024), BF16),
            pltpu.VMEM((rows, 2048), BF16),
            pltpu.VMEM((256, 8 * rows), BF16),
            pltpu.VMEM((8 * rows, ZONES * 256), BF16),
            pltpu.VMEM((kernels.shape[0], PIX, 256), F32),
            pltpu.VMEM((8, rows, 256), F32),
            pltpu.VMEM(cube.shape, F32),
            pltpu.VMEM((height, width), BF16),
            pltpu.VMEM((rows, 128), BF16),
            pltpu.VMEM((2, rows, 128), BF16),
            pltpu.VMEM((rows, 128), F32),
            pltpu.VMEM((2 * PIX, 128), F32),
            pltpu.VMEM((2 * PIX, 128), F32),
            pltpu.VMEM((2 * PIX, 128), F32),
            pltpu.SemaphoreType.DMA((4,)),
            pltpu.SemaphoreType.DMA((4,)),
        ],
        compiler_params=pltpu.CompilerParams(
            collective_id=0, has_side_effects=True, vmem_limit_bytes=50 << 20
        ),
    )(cube, kernels, zone_map, image, kernel_index, step_size, spectral_weight, prior_taps)
    own = lax.dynamic_index_in_dim(
        residual.reshape(tiles, 2, strip, width), lax.axis_index("band"), 1, keepdims=False
    ).reshape(tiles * strip, width)
    return updated, lax.all_to_all(own, "tile", split_axis=0, concat_axis=1, tiled=True)


def solution(mesh):
    return jax.shard_map(
        functools.partial(per_device, mesh.shape["tile"]),
        mesh=mesh,
        in_specs=(
            P(("groups", "band"), None, "tile"),
            P(),
            P(None, "tile"),
            P(),
            P(("groups", "tile", "band"), None),
            P("band"),
            P("band"),
            P(),
        ),
        out_specs=(P(("groups", "band"), None, "tile"), P(("groups", "tile", "band"), None)),
        check_vma=False,
    )
```

```python
import functools

import jax
import jax.numpy as jnp
from jax import lax
from jax.experimental import pallas as pl
from jax.experimental.pallas import tpu as pltpu
from jax.sharding import PartitionSpec as P

BLOCK = 8
SUP = 3
ZONES = 4
PIX = BLOCK * BLOCK
F32 = jnp.float32
BF16 = jnp.bfloat16
MESH = pl.DeviceIdType.MESH
NT = (((1,), (1,)), ((), ()))


def iota(shape, dim):
    return lax.broadcasted_iota(jnp.int32, shape, dim)


def onehot(mask):
    return jnp.where(mask, 1.0, 0.0).astype(BF16)


def dot(a, b):
    return jnp.dot(a, b, preferred_element_type=F32)


def dot_nt(a, b):
    return lax.dot_general(a, b, NT, preferred_element_type=F32)


def kernel(
    tiles, direct,
    cube_hbm, kern_hbm, zone_ref, meas_ref, kidx_ref, step_ref, weight_ref, taps_ref,
    out_ref, res_ref,
    cube_ref, kern_ref, meas_blocks, res_blocks, perm_ref, xcat_ref, at_ref, table_ref, kp_ref, grad_ref, prior_ref,
    edge_ref, hsend_ref, hrecv_ref, halo_ref, mine_ref, theirs_ref, rblk_ref,
    load_sem, send_sem, recv_sem,
):
    bands = cube_ref.shape[0]
    rows = bands * BLOCK
    h = lax.axis_index("band")
    t = lax.axis_index("tile")
    group = lax.axis_index("groups")
    partner = (group, t, 1 - h)
    left = (group, lax.rem(t + tiles - 1, tiles), h)
    right = (group, lax.rem(t + 1, tiles), h)

    load_cube = pltpu.make_async_copy(cube_hbm, cube_ref, load_sem.at[0])
    load_kern = pltpu.make_async_copy(kern_hbm, kern_ref, load_sem.at[1])
    load_cube.start()
    load_kern.start()

    me = 2 * t + h
    count = 2 * tiles
    others = []
    if direct:
        for d in range(1, count):
            peer = lax.rem(me + d, count)
            others.append((peer // 2, (group, peer // 2, lax.rem(peer, 2))))
        greeted = [device for _, device in others]
    else:
        greeted = [partner, left, right]
    barrier = pltpu.get_barrier_semaphore()
    for device in greeted:
        pl.semaphore_signal(barrier, inc=1, device_id=device, device_id_type=MESH)

    for p in range(8):
        n = iota((128, 1024), 0)
        k = iota((128, 1024), 1)
        perm_ref[p * 128 : p * 128 + 128, :] = onehot(k == (n // 16) * 128 + (n % 16) * 8 + p)

    def remote(k, src, dst, device):
        return pltpu.make_async_remote_copy(
            src_ref=src, dst_ref=dst, send_sem=send_sem.at[k], recv_sem=recv_sem.at[k],
            device_id=device, device_id_type=MESH,
        )

    pl.semaphore_wait(barrier, len(greeted))
    copies = [
        remote(0, cube_hbm.at[(bands - 1) * (1 - h)], edge_ref, partner),
        remote(1, hsend_ref, hrecv_ref.at[0], right),
        remote(2, hsend_ref, hrecv_ref.at[1], left),
        remote(3, mine_ref, theirs_ref, partner),
    ]
    copies[0].start()
    meas_copies = [
        remote(
            3 + d,
            meas_ref.at[:, pl.ds(pl.multiple_of(tile * 128, 128), 128)],
            meas_blocks.at[me],
            device,
        )
        for d, (tile, device) in enumerate(others, 1)
    ]
    for copy in meas_copies:
        copy.start()
    if direct:
        load_own = pltpu.make_async_copy(
            meas_ref.at[:, pl.ds(pl.multiple_of(t * 128, 128), 128)],
            meas_blocks.at[me],
            load_sem.at[2],
        )
        load_own.start()

    load_cube.wait()
    for pair in range(8):
        two = cube_ref[:, pair * 16 : pair * 16 + 16, :].astype(F32)
        for k in range(2):
            i = pair * 2 + k
            xcat_ref[:, i * 128 : i * 128 + 128] = (
                two[:, k * 8 : k * 8 + 8].reshape(rows, 128).astype(BF16)
            )

    sel_row = iota((2048, 128), 0)
    sel_lane = iota((2048, 128), 1)
    wanted = (sel_lane // 2) * 128 + jnp.where(sel_lane % 2 == 0, 127, 0)
    hsend_ref[...] = dot(xcat_ref[...], onehot(sel_row == wanted)).astype(BF16)

    copies[1].start()
    copies[2].start()

    for half in range(2):
        blocks = dot_nt(perm_ref[...], xcat_ref[:, half * 1024 : half * 1024 + 1024])
        for p in range(8):
            at_ref[half * 128 : half * 128 + 128, p * rows : p * rows + rows] = blocks[
                p * 128 : p * 128 + 128
            ].astype(BF16)

    load_kern.wait()
    i = iota((256, 256), 0)
    j = iota((256, 256), 1)
    swap = onehot(j == (i // 64) * 64 + (i % 8) * 8 + (i // 8) % 8)
    kp_ref[:, :, 128:256] = jnp.zeros((kp_ref.shape[0], PIX, 128), F32)
    for g in range(kp_ref.shape[0] // 4):
        four = kern_ref[g * 4 : g * 4 + 4].reshape(256, SUP * PIX)
        kp_ref[g * 4 : g * 4 + 4, :, 0 : SUP * PIX] = dot(swap, four).reshape(4, PIX, SUP * PIX)

    def gather(pair, carry):
        for z in range(ZONES):
            first = kp_ref[kidx_ref[z, h * bands + pair * 2]]
            second = kp_ref[kidx_ref[z, h * bands + pair * 2 + 1]]
            for p in range(8):
                chunk = jnp.concatenate(
                    [first[p * 8 : p * 8 + 8], second[p * 8 : p * 8 + 8]], axis=0
                )
                at = pl.multiple_of(p * rows + pair * 16, 16)
                table_ref[pl.ds(at, 16), z * 256 : z * 256 + 256] = chunk.astype(BF16)
        return carry

    lax.fori_loop(0, bands // 2, gather, 0)

    zone = zone_ref[...].astype(F32).astype(BF16)
    spread_col = dot(onehot(iota((256, 16), 0) // 16 == iota((256, 16), 1)), zone)
    keep = iota((256, 16), 0) % 16 == iota((256, 16), 1)
    zone_col = jnp.sum(jnp.where(keep, spread_col, 0.0), axis=1, keepdims=True)
    spread_row = dot(zone, onehot(iota((16, 256), 1) % 16 == iota((16, 256), 0)))
    keep = iota((16, 256), 1) // 16 == iota((16, 256), 0)
    zone_row = jnp.sum(jnp.where(keep, spread_row, 0.0), axis=0, keepdims=True)

    every = dot(at_ref[...], table_ref[...])
    chosen = jnp.zeros((256, 256), F32)
    for z in range(ZONES):
        chosen = jnp.where(zone_col == float(z), every[:, z * 256 : z * 256 + 256], chosen)
    across = chosen.T
    lane = iota((PIX, 256), 1)
    up = pltpu.roll(across[0:PIX], 240, 1)
    down = pltpu.roll(across[2 * PIX : 3 * PIX], 16, 1)
    partial = (
        across[PIX : 2 * PIX]
        + jnp.where(lane < 240, up, 0.0)
        + jnp.where(lane >= 16, down, 0.0)
    )
    for half in range(2):
        mine_ref[half * PIX : half * PIX + PIX, :] = partial[:, half * 128 : half * 128 + 128]
    copies[3].start()

    for copy in copies[:3]:
        copy.wait()
    even = iota((rows, 128), 1) % 2 == 0
    from_left = jnp.where(t > 0, hrecv_ref[0].astype(F32), 0.0)
    from_right = jnp.where(t < tiles - 1, hrecv_ref[1].astype(F32), 0.0)
    halo_ref[...] = jnp.where(even, from_left, from_right)

    lane = iota((128, 128), 1)
    row = iota((128, 128), 0)

    def prior_of(b, carry):
        x = cube_ref[b].astype(F32)
        edge = edge_ref[...].astype(F32)
        before = cube_ref[jnp.maximum(b - 1, 0)].astype(F32)
        after = cube_ref[jnp.minimum(b + 1, bands - 1)].astype(F32)
        before = jnp.where(b > 0, before, jnp.where(h > 0, edge, 0.0))
        after = jnp.where(b < bands - 1, after, jnp.where(h < 1, edge, 0.0))
        one = halo_ref[pl.ds(pl.multiple_of(b * 8, 8), 8), :]
        rim = jnp.concatenate(
            [pltpu.roll(one, 127 - 2 * i, 1) for i in range(16)], axis=0
        )
        west = pltpu.roll(jnp.where(lane == 127, rim, x), 1, 1)
        east = pltpu.roll(jnp.where(lane == 0, rim, x), 127, 1)
        terms = [
            taps_ref[a, 0] * west + taps_ref[a, 1] * x + taps_ref[a, 2] * east
            for a in range(3)
        ]
        spatial = (
            terms[1]
            + jnp.where(row > 0, pltpu.roll(terms[0], 1, 0), 0.0)
            + jnp.where(row < 127, pltpu.roll(terms[2], 127, 0), 0.0)
        )
        prior_ref[b] = spatial + weight_ref[b] * (2.0 * x - before - after)
        return carry

    lax.fori_loop(0, bands, prior_of, 0)

    copies[3].wait()
    mine_ref[...] = mine_ref[...] + theirs_ref[...]
    flat = jnp.concatenate(
        [
            jnp.concatenate(
                [
                    mine_ref[pl.ds(half * PIX + q, 8, stride=8), :]
                    for q in range(8)
                ],
                axis=1,
            )
            for half in range(2)
        ],
        axis=0,
    )
    high = flat.astype(BF16)
    rest = flat - high.astype(F32)
    mid = rest.astype(BF16)
    low = (rest - mid.astype(F32)).astype(BF16)
    parts = dot(jnp.concatenate([high, mid, low], axis=0), perm_ref[...])
    image = parts[0:16] + (parts[16:32] + parts[32:48])
    if direct:
        load_own.wait()
        for copy in meas_copies:
            copy.wait()
    residual = []
    for i in range(16):
        half, k = i // 8, i % 8
        piece = image[half * 8 : half * 8 + 8, k * 128 : k * 128 + 128]
        if direct:
            piece = piece - meas_blocks[i]
            res_blocks[i] = piece
        else:
            piece = piece - meas_ref[i * 8 : i * 8 + 8, :]
            res_ref[i * 8 : i * 8 + 8, :] = piece
        residual.append(piece)
    res_copies = []
    if direct:
        own = pl.ds(pl.multiple_of(t * 128, 128), 128)
        for d in range(1, tiles):
            tile = lax.rem(t + d, tiles)
            res_copies.append(
                remote(
                    2 + count + d, res_blocks.at[2 * tile + h], res_ref.at[:, own], (group, tile, h)
                )
            )
        for copy in res_copies:
            copy.start()
        res_ref[:, own] = res_blocks[me]
    flat = jnp.concatenate(
        [jnp.concatenate(residual[half * 8 : half * 8 + 8], axis=1) for half in range(2)], axis=0
    ).astype(BF16)
    back = dot_nt(flat, perm_ref[...])
    for half in range(2):
        for q in range(8):
            rblk_ref[pl.ds(half * PIX + q, 8, stride=8), :] = back[
                half * 8 : half * 8 + 8, q * 128 : q * 128 + 128
            ]
    centre = jnp.concatenate([rblk_ref[0:PIX, :], rblk_ref[PIX : 2 * PIX, :]], axis=1)
    lane = iota((PIX, 256), 1)
    above = jnp.where(lane >= 16, pltpu.roll(centre, 16, 1), 0.0)
    below = jnp.where(lane < 240, pltpu.roll(centre, 240, 1), 0.0)
    stacked = jnp.concatenate([above, centre, below, jnp.zeros((PIX, 256), F32)], axis=0)
    zoned = jnp.concatenate(
        [jnp.where(zone_row == float(z), stacked, 0.0) for z in range(ZONES)], axis=0
    ).astype(BF16)

    for p in range(8):
        grad_ref[p] = dot(table_ref[p * rows : p * rows + rows, :], zoned)
    for half in range(2):
        wide = jnp.concatenate(
            [grad_ref[p, :, half * 128 : half * 128 + 128] for p in range(8)], axis=1
        )
        high = wide.astype(BF16)
        low = (wide - high.astype(F32)).astype(BF16)
        gradient = dot(high, perm_ref[...]) + dot(low, perm_ref[...])
        for k in range(8):
            i = half * 8 + k
            prior_ref[:, i * 8 : i * 8 + 8, :] = prior_ref[:, i * 8 : i * 8 + 8, :] + gradient[
                :, k * 128 : k * 128 + 128
            ].reshape(bands, 8, 128)

    def update(b, carry):
        out_ref[b] = (cube_ref[b].astype(F32) - step_ref[b] * prior_ref[b]).astype(BF16)
        return carry

    lax.fori_loop(0, bands, update, 0)
    for copy in res_copies:
        copy.wait()


def per_device(
    tiles, cube, kernels, zone_map, kernel_index, measurement, step_size, spectral_weight,
    prior_taps,
):
    bands, height, width = cube.shape
    strip = measurement.shape[0]
    rows = bands * BLOCK
    direct = strip == BLOCK and width == 128
    if direct:
        image = measurement
        sems = 3 + 2 * tiles + tiles
    else:
        moved = lax.all_to_all(measurement, "tile", split_axis=1, concat_axis=0, tiled=True)
        both = lax.all_gather(moved, "band", axis=0, tiled=False)
        image = both.reshape(2, tiles, strip, width).transpose(1, 0, 2, 3).reshape(height, width)
        sems = 4
    hbm = pl.BlockSpec(memory_space=pltpu.HBM)
    vmem = pl.BlockSpec(memory_space=pltpu.VMEM)
    smem = pl.BlockSpec(memory_space=pltpu.SMEM)
    updated, residual = pl.pallas_call(
        functools.partial(kernel, tiles, direct),
        out_shape=(
            jax.ShapeDtypeStruct(cube.shape, BF16),
            jax.ShapeDtypeStruct(image.shape, F32),
        ),
        in_specs=[hbm, hbm, vmem, hbm if direct else vmem] + [smem] * 4,
        out_specs=(vmem, vmem),
        scratch_shapes=[
            pltpu.VMEM(cube.shape, BF16),
            pltpu.VMEM(kernels.shape, BF16),
            pltpu.VMEM((height // BLOCK, BLOCK, width), F32),
            pltpu.VMEM((height // BLOCK, BLOCK, width), F32),
            pltpu.VMEM((1024, 1024), BF16),
            pltpu.VMEM((rows, 2048), BF16),
            pltpu.VMEM((256, 8 * rows), BF16),
            pltpu.VMEM((8 * rows, ZONES * 256), BF16),
            pltpu.VMEM((kernels.shape[0], PIX, 256), F32),
            pltpu.VMEM((8, rows, 256), F32),
            pltpu.VMEM(cube.shape, F32),
            pltpu.VMEM((height, width), BF16),
            pltpu.VMEM((rows, 128), BF16),
            pltpu.VMEM((2, rows, 128), BF16),
            pltpu.VMEM((rows, 128), F32),
            pltpu.VMEM((2 * PIX, 128), F32),
            pltpu.VMEM((2 * PIX, 128), F32),
            pltpu.VMEM((2 * PIX, 128), F32),
            pltpu.SemaphoreType.DMA((3,)),
            pltpu.SemaphoreType.DMA((sems,)),
            pltpu.SemaphoreType.DMA((sems,)),
        ],
        compiler_params=pltpu.CompilerParams(
            collective_id=0, has_side_effects=True, vmem_limit_bytes=50 << 20
        ),
    )(cube, kernels, zone_map, image, kernel_index.T, step_size, spectral_weight, prior_taps)
    if direct:
        return updated, residual
    own = lax.dynamic_index_in_dim(
        residual.reshape(tiles, 2, strip, width), lax.axis_index("band"), 1, keepdims=False
    ).reshape(tiles * strip, width)
    return updated, lax.all_to_all(own, "tile", split_axis=0, concat_axis=1, tiled=True)


def solution(mesh):
    return jax.shard_map(
        functools.partial(per_device, mesh.shape["tile"]),
        mesh=mesh,
        in_specs=(
            P(("groups", "band"), None, "tile"),
            P(),
            P(None, "tile"),
            P(),
            P(("groups", "tile", "band"), None),
            P("band"),
            P("band"),
            P(),
        ),
        out_specs=(P(("groups", "band"), None, "tile"), P(("groups", "tile", "band"), None)),
        check_vma=False,
    )
```

```python
import functools

import jax
import jax.numpy as jnp
from jax import lax
from jax.experimental import pallas as pl
from jax.experimental.pallas import tpu as pltpu
from jax.sharding import PartitionSpec as P

BLOCK = 8
SUP = 3
ZONES = 4
PIX = BLOCK * BLOCK
F32 = jnp.float32
BF16 = jnp.bfloat16
MESH = pl.DeviceIdType.MESH
NT = (((1,), (1,)), ((), ()))


def iota(shape, dim):
    return lax.broadcasted_iota(jnp.int32, shape, dim)


def onehot(mask):
    return jnp.where(mask, 1.0, 0.0).astype(BF16)


def dot(a, b):
    return jnp.dot(a, b, preferred_element_type=F32)


def dot_nt(a, b):
    return lax.dot_general(a, b, NT, preferred_element_type=F32)


def kernel(
    tiles, direct,
    cube_hbm, kern_hbm, zone_ref, meas_ref, kidx_ref, step_ref, weight_ref, taps_ref,
    out_hbm, res_ref,
    cube_ref, new_ref, grows_ref, rowtaps_ref, along_ref, kern_ref, meas_blocks, res_blocks, perm_ref, xcat_ref, at_ref, table_ref, kp_ref, grad_ref, prior_ref,
    edge_ref, hsend_ref, hrecv_ref, halo_ref, mine_ref, theirs_ref, rblk_ref,
    load_sem, send_sem, recv_sem,
):
    bands = cube_ref.shape[0]
    rows = bands * BLOCK
    h = lax.axis_index("band")
    t = lax.axis_index("tile")
    group = lax.axis_index("groups")
    partner = (group, t, 1 - h)
    left = (group, lax.rem(t + tiles - 1, tiles), h)
    right = (group, lax.rem(t + 1, tiles), h)

    load_cube = pltpu.make_async_copy(cube_hbm, cube_ref, load_sem.at[0])
    load_kern = pltpu.make_async_copy(kern_hbm, kern_ref, load_sem.at[1])
    load_cube.start()
    load_kern.start()

    me = 2 * t + h
    count = 2 * tiles
    others = []
    if direct:
        for d in range(1, count):
            peer = lax.rem(me + d, count)
            others.append((peer // 2, (group, peer // 2, lax.rem(peer, 2))))
        greeted = [device for _, device in others]
    else:
        greeted = [partner, left, right]
    barrier = pltpu.get_barrier_semaphore()
    for device in greeted:
        pl.semaphore_signal(barrier, inc=1, device_id=device, device_id_type=MESH)

    for p in range(8):
        n = iota((128, 1024), 0)
        k = iota((128, 1024), 1)
        perm_ref[p * 128 : p * 128 + 128, :] = onehot(k == (n // 16) * 128 + (n % 16) * 8 + p)

    def remote(k, src, dst, device):
        return pltpu.make_async_remote_copy(
            src_ref=src, dst_ref=dst, send_sem=send_sem.at[k], recv_sem=recv_sem.at[k],
            device_id=device, device_id_type=MESH,
        )

    pl.semaphore_wait(barrier, len(greeted))
    copies = [
        remote(0, cube_hbm.at[(bands - 1) * (1 - h)], edge_ref, partner),
        remote(1, hsend_ref, hrecv_ref.at[0], right),
        remote(2, hsend_ref, hrecv_ref.at[1], left),
        remote(3, mine_ref, theirs_ref, partner),
    ]
    copies[0].start()
    meas_copies = [
        remote(
            3 + d,
            meas_ref.at[:, pl.ds(pl.multiple_of(tile * 128, 128), 128)],
            meas_blocks.at[me],
            device,
        )
        for d, (tile, device) in enumerate(others, 1)
    ]
    for copy in meas_copies:
        copy.start()
    if direct:
        load_own = pltpu.make_async_copy(
            meas_ref.at[:, pl.ds(pl.multiple_of(t * 128, 128), 128)],
            meas_blocks.at[me],
            load_sem.at[2],
        )
        load_own.start()

    load_cube.wait()
    for pair in range(8):
        two = cube_ref[:, pair * 16 : pair * 16 + 16, :].astype(F32)
        for k in range(2):
            i = pair * 2 + k
            xcat_ref[:, i * 128 : i * 128 + 128] = (
                two[:, k * 8 : k * 8 + 8].reshape(rows, 128).astype(BF16)
            )

    sel_row = iota((2048, 128), 0)
    sel_lane = iota((2048, 128), 1)
    wanted = (sel_lane // 2) * 128 + jnp.where(sel_lane % 2 == 0, 127, 0)
    hsend_ref[...] = dot(xcat_ref[...], onehot(sel_row == wanted)).astype(BF16)

    copies[1].start()
    copies[2].start()

    for half in range(2):
        blocks = dot_nt(perm_ref[...], xcat_ref[:, half * 1024 : half * 1024 + 1024])
        for p in range(8):
            at_ref[half * 128 : half * 128 + 128, p * rows : p * rows + rows] = blocks[
                p * 128 : p * 128 + 128
            ].astype(BF16)

    load_kern.wait()
    i = iota((256, 256), 0)
    j = iota((256, 256), 1)
    swap = onehot(j == (i // 64) * 64 + (i % 8) * 8 + (i // 8) % 8)
    kp_ref[:, :, 128:256] = jnp.zeros((kp_ref.shape[0], PIX, 128), F32)
    for g in range(kp_ref.shape[0] // 4):
        four = kern_ref[g * 4 : g * 4 + 4].reshape(256, SUP * PIX)
        kp_ref[g * 4 : g * 4 + 4, :, 0 : SUP * PIX] = dot(swap, four).reshape(4, PIX, SUP * PIX)

    def gather(pair, carry):
        for z in range(ZONES):
            first = kp_ref[kidx_ref[z, h * bands + pair * 2]]
            second = kp_ref[kidx_ref[z, h * bands + pair * 2 + 1]]
            for p in range(8):
                chunk = jnp.concatenate(
                    [first[p * 8 : p * 8 + 8], second[p * 8 : p * 8 + 8]], axis=0
                )
                at = pl.multiple_of(p * rows + pair * 16, 16)
                table_ref[pl.ds(at, 16), z * 256 : z * 256 + 256] = chunk.astype(BF16)
        return carry

    lax.fori_loop(0, bands // 2, gather, 0)

    zone = zone_ref[...].astype(F32).astype(BF16)
    spread_col = dot(onehot(iota((256, 16), 0) // 16 == iota((256, 16), 1)), zone)
    keep = iota((256, 16), 0) % 16 == iota((256, 16), 1)
    zone_col = jnp.sum(jnp.where(keep, spread_col, 0.0), axis=1, keepdims=True)
    spread_row = dot(zone, onehot(iota((16, 256), 1) % 16 == iota((16, 256), 0)))
    keep = iota((16, 256), 1) // 16 == iota((16, 256), 0)
    zone_row = jnp.sum(jnp.where(keep, spread_row, 0.0), axis=0, keepdims=True)

    every = dot(at_ref[...], table_ref[...])
    chosen = jnp.zeros((256, 256), F32)
    for z in range(ZONES):
        chosen = jnp.where(zone_col == float(z), every[:, z * 256 : z * 256 + 256], chosen)
    across = chosen.T
    lane = iota((PIX, 256), 1)
    up = pltpu.roll(across[0:PIX], 240, 1)
    down = pltpu.roll(across[2 * PIX : 3 * PIX], 16, 1)
    partial = (
        across[PIX : 2 * PIX]
        + jnp.where(lane < 240, up, 0.0)
        + jnp.where(lane >= 16, down, 0.0)
    )
    for half in range(2):
        mine_ref[half * PIX : half * PIX + PIX, :] = partial[:, half * 128 : half * 128 + 128]
    copies[3].start()

    for copy in copies[:3]:
        copy.wait()
    even = iota((rows, 128), 1) % 2 == 0
    from_left = jnp.where(t > 0, hrecv_ref[0].astype(F32), 0.0)
    from_right = jnp.where(t < tiles - 1, hrecv_ref[1].astype(F32), 0.0)
    halo_ref[...] = jnp.where(even, from_left, from_right)

    source = iota((128, 128), 0)
    target = iota((128, 128), 1)
    for a in range(3):
        first, centre, last = taps_ref[a, 0], taps_ref[a, 1], taps_ref[a, 2]
        inner = (
            jnp.where(source == target - 1, first, 0.0)
            + jnp.where(source == target, centre, 0.0)
            + jnp.where(source == target + 1, last, 0.0)
        )
        outer = jnp.where((target == 0) & (source % 2 == 0), first, 0.0) + jnp.where(
            (target == 127) & (source % 2 == 1), last, 0.0
        )
        taps = jnp.concatenate([inner, outer], axis=0)
        high = taps.astype(BF16)
        low = (taps - high.astype(F32)).astype(BF16)
        rowtaps_ref[0:256, a * 128 : a * 128 + 128] = high
        rowtaps_ref[256:512, a * 128 : a * 128 + 128] = low

    row = iota((128, 128), 0)
    edge = edge_ref[...].astype(F32)
    owner = iota((16, 8, 128), 2) // 2 == iota((16, 8, 128), 0)
    for g in range(bands // 8):
        inside = cube_ref[g * 8 : g * 8 + 8].reshape(1024, 128)
        rim = halo_ref[g * 64 : g * 64 + 64, :].reshape(8, 1, 8, 128)
        rim = jnp.where(owner[None], rim, 0.0).reshape(1024, 128).astype(BF16)
        along_ref[...] = dot(
            jnp.concatenate([inside, rim, inside, rim], axis=1), rowtaps_ref[...]
        )
        for k in range(8):
            b = g * 8 + k
            x = cube_ref[b].astype(F32)
            if b > 0:
                before = cube_ref[b - 1].astype(F32)
            else:
                before = jnp.where(h > 0, edge, 0.0)
            if b < bands - 1:
                after = cube_ref[b + 1].astype(F32)
            else:
                after = jnp.where(h < 1, edge, 0.0)
            span = slice(k * 128, k * 128 + 128)
            spatial = (
                along_ref[span, 128:256]
                + jnp.where(row > 0, pltpu.roll(along_ref[span, 0:128], 1, 0), 0.0)
                + jnp.where(row < 127, pltpu.roll(along_ref[span, 256:384], 127, 0), 0.0)
            )
            prior_ref[b] = spatial + weight_ref[b] * (2.0 * x - before - after)

    copies[3].wait()
    mine_ref[...] = mine_ref[...] + theirs_ref[...]
    flat = jnp.concatenate(
        [
            jnp.concatenate(
                [
                    mine_ref[pl.ds(half * PIX + q, 8, stride=8), :]
                    for q in range(8)
                ],
                axis=1,
            )
            for half in range(2)
        ],
        axis=0,
    )
    high = flat.astype(BF16)
    rest = flat - high.astype(F32)
    mid = rest.astype(BF16)
    low = (rest - mid.astype(F32)).astype(BF16)
    parts = dot(jnp.concatenate([high, mid, low], axis=0), perm_ref[...])
    image = parts[0:16] + (parts[16:32] + parts[32:48])
    if direct:
        load_own.wait()
        for copy in meas_copies:
            copy.wait()
    residual = []
    for i in range(16):
        half, k = i // 8, i % 8
        piece = image[half * 8 : half * 8 + 8, k * 128 : k * 128 + 128]
        if direct:
            piece = piece - meas_blocks[i]
            res_blocks[i] = piece
        else:
            piece = piece - meas_ref[i * 8 : i * 8 + 8, :]
            res_ref[i * 8 : i * 8 + 8, :] = piece
        residual.append(piece)
    res_copies = []
    if direct:
        own = pl.ds(pl.multiple_of(t * 128, 128), 128)
        for d in range(1, tiles):
            tile = lax.rem(t + d, tiles)
            res_copies.append(
                remote(
                    2 + count + d, res_blocks.at[2 * tile + h], res_ref.at[:, own], (group, tile, h)
                )
            )
        for copy in res_copies:
            copy.start()
        res_ref[:, own] = res_blocks[me]
    flat = jnp.concatenate(
        [jnp.concatenate(residual[half * 8 : half * 8 + 8], axis=1) for half in range(2)], axis=0
    ).astype(BF16)
    back = dot_nt(flat, perm_ref[...])
    for half in range(2):
        for q in range(8):
            rblk_ref[pl.ds(half * PIX + q, 8, stride=8), :] = back[
                half * 8 : half * 8 + 8, q * 128 : q * 128 + 128
            ]
    centre = jnp.concatenate([rblk_ref[0:PIX, :], rblk_ref[PIX : 2 * PIX, :]], axis=1)
    lane = iota((PIX, 256), 1)
    above = jnp.where(lane >= 16, pltpu.roll(centre, 16, 1), 0.0)
    below = jnp.where(lane < 240, pltpu.roll(centre, 240, 1), 0.0)
    stacked = jnp.concatenate([above, centre, below, jnp.zeros((PIX, 256), F32)], axis=0)
    zoned = jnp.concatenate(
        [jnp.where(zone_row == float(z), stacked, 0.0) for z in range(ZONES)], axis=0
    ).astype(BF16)

    for p in range(8):
        grad_ref[p] = dot(table_ref[p * rows : p * rows + rows, :], zoned)
    stores = []
    for half in range(2):
        wide = jnp.concatenate(
            [grad_ref[p, :, half * 128 : half * 128 + 128] for p in range(8)], axis=1
        )
        high = wide.astype(BF16)
        low = (wide - high.astype(F32)).astype(BF16)
        grows_ref[...] = dot(high, perm_ref[...]) + dot(low, perm_ref[...])
        span = slice(half * 64, half * 64 + 64)

        def update(b, carry):
            at = pl.ds(pl.multiple_of(b * 8, 8), 8)
            gradient = jnp.concatenate(
                [grows_ref[at, k * 128 : k * 128 + 128] for k in range(8)], axis=0
            )
            total = gradient + prior_ref[b, span]
            new_ref[b, span] = (cube_ref[b, span].astype(F32) - step_ref[b] * total).astype(BF16)
            return carry

        lax.fori_loop(0, bands, update, 0, unroll=4)
        store = pltpu.make_async_copy(
            new_ref.at[:, span], out_hbm.at[:, span], load_sem.at[3 + half]
        )
        store.start()
        stores.append(store)
    for store in stores:
        store.wait()
    for copy in res_copies:
        copy.wait()


def per_device(
    tiles, cube, kernels, zone_map, kernel_index, measurement, step_size, spectral_weight,
    prior_taps,
):
    bands, height, width = cube.shape
    strip = measurement.shape[0]
    rows = bands * BLOCK
    direct = strip == BLOCK and width == 128
    if direct:
        image = measurement
        sems = 3 + 2 * tiles + tiles
    else:
        moved = lax.all_to_all(measurement, "tile", split_axis=1, concat_axis=0, tiled=True)
        both = lax.all_gather(moved, "band", axis=0, tiled=False)
        image = both.reshape(2, tiles, strip, width).transpose(1, 0, 2, 3).reshape(height, width)
        sems = 4
    hbm = pl.BlockSpec(memory_space=pltpu.HBM)
    vmem = pl.BlockSpec(memory_space=pltpu.VMEM)
    smem = pl.BlockSpec(memory_space=pltpu.SMEM)
    updated, residual = pl.pallas_call(
        functools.partial(kernel, tiles, direct),
        out_shape=(
            jax.ShapeDtypeStruct(cube.shape, BF16),
            jax.ShapeDtypeStruct(image.shape, F32),
        ),
        in_specs=[hbm, hbm, vmem, hbm if direct else vmem] + [smem] * 4,
        out_specs=(hbm, vmem),
        scratch_shapes=[
            pltpu.VMEM(cube.shape, BF16),
            pltpu.VMEM(cube.shape, BF16),
            pltpu.VMEM((rows, 1024), F32),
            pltpu.VMEM((512, 384), BF16),
            pltpu.VMEM((1024, 384), F32),
            pltpu.VMEM(kernels.shape, BF16),
            pltpu.VMEM((height // BLOCK, BLOCK, width), F32),
            pltpu.VMEM((height // BLOCK, BLOCK, width), F32),
            pltpu.VMEM((1024, 1024), BF16),
            pltpu.VMEM((rows, 2048), BF16),
            pltpu.VMEM((256, 8 * rows), BF16),
            pltpu.VMEM((8 * rows, ZONES * 256), BF16),
            pltpu.VMEM((kernels.shape[0], PIX, 256), F32),
            pltpu.VMEM((8, rows, 256), F32),
            pltpu.VMEM(cube.shape, F32),
            pltpu.VMEM((height, width), BF16),
            pltpu.VMEM((rows, 128), BF16),
            pltpu.VMEM((2, rows, 128), BF16),
            pltpu.VMEM((rows, 128), F32),
            pltpu.VMEM((2 * PIX, 128), F32),
            pltpu.VMEM((2 * PIX, 128), F32),
            pltpu.VMEM((2 * PIX, 128), F32),
            pltpu.SemaphoreType.DMA((5,)),
            pltpu.SemaphoreType.DMA((sems,)),
            pltpu.SemaphoreType.DMA((sems,)),
        ],
        compiler_params=pltpu.CompilerParams(
            collective_id=0, has_side_effects=True, vmem_limit_bytes=62 << 20
        ),
    )(cube, kernels, zone_map, image, kernel_index.T, step_size, spectral_weight, prior_taps)
    if direct:
        return updated, residual
    own = lax.dynamic_index_in_dim(
        residual.reshape(tiles, 2, strip, width), lax.axis_index("band"), 1, keepdims=False
    ).reshape(tiles * strip, width)
    return updated, lax.all_to_all(own, "tile", split_axis=0, concat_axis=1, tiled=True)


def solution(mesh):
    return jax.shard_map(
        functools.partial(per_device, mesh.shape["tile"]),
        mesh=mesh,
        in_specs=(
            P(("groups", "band"), None, "tile"),
            P(),
            P(None, "tile"),
            P(),
            P(("groups", "tile", "band"), None),
            P("band"),
            P("band"),
            P(),
        ),
        out_specs=(P(("groups", "band"), None, "tile"), P(("groups", "tile", "band"), None)),
        check_vma=False,
    )
```

```python
import functools

import jax
import jax.numpy as jnp
from jax import lax
from jax.experimental import pallas as pl
from jax.experimental.pallas import tpu as pltpu
from jax.sharding import PartitionSpec as P

BLOCK = 8
SUP = 3
ZONES = 4
PIX = BLOCK * BLOCK
F32 = jnp.float32
BF16 = jnp.bfloat16
MESH = pl.DeviceIdType.MESH
NT = (((1,), (1,)), ((), ()))


def iota(shape, dim):
    return lax.broadcasted_iota(jnp.int32, shape, dim)


def onehot(mask):
    return jnp.where(mask, 1.0, 0.0).astype(BF16)


def dot(a, b):
    return jnp.dot(a, b, preferred_element_type=F32)


def dot_nt(a, b):
    return lax.dot_general(a, b, NT, preferred_element_type=F32)


def kernel(
    tiles, direct,
    cube_hbm, kern_hbm, zone_ref, meas_ref, kidx_ref, step_ref, weight_ref, taps_ref,
    out_hbm, res_ref,
    cube_ref, new_ref, grows_ref, rowtaps_ref, along_ref, kern_ref, meas_blocks, res_blocks, perm_ref, xcat_ref, at_ref, table_ref, kp_ref, grad_ref, prior_ref,
    edge_ref, hsend_ref, hrecv_ref, halo_ref, mine_ref, theirs_ref, rblk_ref,
    load_sem, send_sem, recv_sem,
):
    bands = cube_ref.shape[0]
    rows = bands * BLOCK
    h = lax.axis_index("band")
    t = lax.axis_index("tile")
    group = lax.axis_index("groups")
    partner = (group, t, 1 - h)
    left = (group, lax.rem(t + tiles - 1, tiles), h)
    right = (group, lax.rem(t + 1, tiles), h)

    load_cube = pltpu.make_async_copy(cube_hbm, cube_ref, load_sem.at[0])
    load_kern = pltpu.make_async_copy(kern_hbm, kern_ref, load_sem.at[1])
    load_cube.start()
    load_kern.start()

    me = 2 * t + h
    count = 2 * tiles
    others = []
    if direct:
        for d in range(1, count):
            peer = lax.rem(me + d, count)
            others.append((peer // 2, (group, peer // 2, lax.rem(peer, 2))))
        greeted = [device for _, device in others]
    else:
        greeted = [partner, left, right]
    barrier = pltpu.get_barrier_semaphore()
    for device in greeted:
        pl.semaphore_signal(barrier, inc=1, device_id=device, device_id_type=MESH)

    for p in range(8):
        n = iota((128, 1024), 0)
        k = iota((128, 1024), 1)
        perm_ref[p * 128 : p * 128 + 128, :] = onehot(k == (n // 16) * 128 + (n % 16) * 8 + p)

    def remote(k, src, dst, device):
        return pltpu.make_async_remote_copy(
            src_ref=src, dst_ref=dst, send_sem=send_sem.at[k], recv_sem=recv_sem.at[k],
            device_id=device, device_id_type=MESH,
        )

    load_cube.wait()
    for pair in range(8):
        two = cube_ref[:, pair * 16 : pair * 16 + 16, :].astype(F32)
        for k in range(2):
            i = pair * 2 + k
            xcat_ref[:, i * 128 : i * 128 + 128] = (
                two[:, k * 8 : k * 8 + 8].reshape(rows, 128).astype(BF16)
            )

    sel_row = iota((2048, 128), 0)
    sel_lane = iota((2048, 128), 1)
    wanted = (sel_lane // 2) * 128 + jnp.where(sel_lane % 2 == 0, 127, 0)
    hsend_ref[...] = dot(xcat_ref[...], onehot(sel_row == wanted)).astype(BF16)

    pl.semaphore_wait(barrier, len(greeted))
    copies = [
        remote(0, cube_hbm.at[(bands - 1) * (1 - h)], edge_ref, partner),
        remote(1, hsend_ref, hrecv_ref.at[0], right),
        remote(2, hsend_ref, hrecv_ref.at[1], left),
        remote(3, mine_ref, theirs_ref, partner),
    ]
    copies[1].start()
    copies[2].start()
    copies[0].start()
    meas_copies = [
        remote(
            3 + d,
            meas_ref.at[:, pl.ds(pl.multiple_of(tile * 128, 128), 128)],
            meas_blocks.at[me],
            device,
        )
        for d, (tile, device) in enumerate(others, 1)
    ]
    for copy in meas_copies:
        copy.start()
    if direct:
        load_own = pltpu.make_async_copy(
            meas_ref.at[:, pl.ds(pl.multiple_of(t * 128, 128), 128)],
            meas_blocks.at[me],
            load_sem.at[2],
        )
        load_own.start()

    for half in range(2):
        blocks = dot_nt(perm_ref[...], xcat_ref[:, half * 1024 : half * 1024 + 1024])
        for p in range(8):
            at_ref[half * 128 : half * 128 + 128, p * rows : p * rows + rows] = blocks[
                p * 128 : p * 128 + 128
            ].astype(BF16)

    load_kern.wait()
    i = iota((256, 256), 0)
    j = iota((256, 256), 1)
    swap = onehot(j == (i // 64) * 64 + (i % 8) * 8 + (i // 8) % 8)
    kp_ref[:, :, 128:256] = jnp.zeros((kp_ref.shape[0], PIX, 128), F32)
    for g in range(kp_ref.shape[0] // 4):
        four = kern_ref[g * 4 : g * 4 + 4].reshape(256, SUP * PIX)
        kp_ref[g * 4 : g * 4 + 4, :, 0 : SUP * PIX] = dot(swap, four).reshape(4, PIX, SUP * PIX)

    def gather(pair, carry):
        for z in range(ZONES):
            first = kp_ref[kidx_ref[z, h * bands + pair * 2]]
            second = kp_ref[kidx_ref[z, h * bands + pair * 2 + 1]]
            for p in range(8):
                chunk = jnp.concatenate(
                    [first[p * 8 : p * 8 + 8], second[p * 8 : p * 8 + 8]], axis=0
                )
                at = pl.multiple_of(p * rows + pair * 16, 16)
                table_ref[pl.ds(at, 16), z * 256 : z * 256 + 256] = chunk.astype(BF16)
        return carry

    lax.fori_loop(0, bands // 2, gather, 0)

    zone = zone_ref[...].astype(F32).astype(BF16)
    spread_col = dot(onehot(iota((256, 16), 0) // 16 == iota((256, 16), 1)), zone)
    keep = iota((256, 16), 0) % 16 == iota((256, 16), 1)
    zone_col = jnp.sum(jnp.where(keep, spread_col, 0.0), axis=1, keepdims=True)
    spread_row = dot(zone, onehot(iota((16, 256), 1) % 16 == iota((16, 256), 0)))
    keep = iota((16, 256), 1) // 16 == iota((16, 256), 0)
    zone_row = jnp.sum(jnp.where(keep, spread_row, 0.0), axis=0, keepdims=True)

    every = dot(at_ref[...], table_ref[...])
    chosen = jnp.zeros((256, 256), F32)
    for z in range(ZONES):
        chosen = jnp.where(zone_col == float(z), every[:, z * 256 : z * 256 + 256], chosen)
    across = chosen.T
    lane = iota((PIX, 256), 1)
    up = pltpu.roll(across[0:PIX], 240, 1)
    down = pltpu.roll(across[2 * PIX : 3 * PIX], 16, 1)
    partial = (
        across[PIX : 2 * PIX]
        + jnp.where(lane < 240, up, 0.0)
        + jnp.where(lane >= 16, down, 0.0)
    )
    for half in range(2):
        mine_ref[half * PIX : half * PIX + PIX, :] = partial[:, half * 128 : half * 128 + 128]
    copies[3].start()

    for copy in copies[:3]:
        copy.wait()
    even = iota((rows, 128), 1) % 2 == 0
    from_left = jnp.where(t > 0, hrecv_ref[0].astype(F32), 0.0)
    from_right = jnp.where(t < tiles - 1, hrecv_ref[1].astype(F32), 0.0)
    halo_ref[...] = jnp.where(even, from_left, from_right)

    source = iota((128, 128), 0)
    target = iota((128, 128), 1)
    for a in range(3):
        first, centre, last = taps_ref[a, 0], taps_ref[a, 1], taps_ref[a, 2]
        inner = (
            jnp.where(source == target - 1, first, 0.0)
            + jnp.where(source == target, centre, 0.0)
            + jnp.where(source == target + 1, last, 0.0)
        )
        outer = jnp.where((target == 0) & (source % 2 == 0), first, 0.0) + jnp.where(
            (target == 127) & (source % 2 == 1), last, 0.0
        )
        taps = jnp.concatenate([inner, outer], axis=0)
        high = taps.astype(BF16)
        low = (taps - high.astype(F32)).astype(BF16)
        rowtaps_ref[0:256, a * 128 : a * 128 + 128] = high
        rowtaps_ref[256:512, a * 128 : a * 128 + 128] = low

    row = iota((128, 128), 0)
    edge = edge_ref[...].astype(F32)
    owner = iota((16, 8, 128), 2) // 2 == iota((16, 8, 128), 0)
    for g in range(bands // 8):
        inside = cube_ref[g * 8 : g * 8 + 8].reshape(1024, 128)
        rim = halo_ref[g * 64 : g * 64 + 64, :].reshape(8, 1, 8, 128)
        rim = jnp.where(owner[None], rim, 0.0).reshape(1024, 128).astype(BF16)
        along_ref[...] = dot(
            jnp.concatenate([inside, rim, inside, rim], axis=1), rowtaps_ref[...]
        )
        for k in range(8):
            b = g * 8 + k
            x = cube_ref[b].astype(F32)
            if b > 0:
                before = cube_ref[b - 1].astype(F32)
            else:
                before = jnp.where(h > 0, edge, 0.0)
            if b < bands - 1:
                after = cube_ref[b + 1].astype(F32)
            else:
                after = jnp.where(h < 1, edge, 0.0)
            span = slice(k * 128, k * 128 + 128)
            spatial = (
                along_ref[span, 128:256]
                + jnp.where(row > 0, pltpu.roll(along_ref[span, 0:128], 1, 0), 0.0)
                + jnp.where(row < 127, pltpu.roll(along_ref[span, 256:384], 127, 0), 0.0)
            )
            prior_ref[b] = spatial + weight_ref[b] * (2.0 * x - before - after)

    copies[3].wait()
    mine_ref[...] = mine_ref[...] + theirs_ref[...]
    flat = jnp.concatenate(
        [
            jnp.concatenate(
                [
                    mine_ref[pl.ds(half * PIX + q, 8, stride=8), :]
                    for q in range(8)
                ],
                axis=1,
            )
            for half in range(2)
        ],
        axis=0,
    )
    high = flat.astype(BF16)
    rest = flat - high.astype(F32)
    mid = rest.astype(BF16)
    low = (rest - mid.astype(F32)).astype(BF16)
    parts = dot(jnp.concatenate([high, mid, low], axis=0), perm_ref[...])
    image = parts[0:16] + (parts[16:32] + parts[32:48])
    if direct:
        load_own.wait()
        for copy in meas_copies:
            copy.wait()
    residual = []
    for i in range(16):
        half, k = i // 8, i % 8
        piece = image[half * 8 : half * 8 + 8, k * 128 : k * 128 + 128]
        if direct:
            piece = piece - meas_blocks[i]
            res_blocks[i] = piece
        else:
            piece = piece - meas_ref[i * 8 : i * 8 + 8, :]
            res_ref[i * 8 : i * 8 + 8, :] = piece
        residual.append(piece)
    res_copies = []
    if direct:
        own = pl.ds(pl.multiple_of(t * 128, 128), 128)
        for d in range(1, tiles):
            tile = lax.rem(t + d, tiles)
            res_copies.append(
                remote(
                    2 + count + d, res_blocks.at[2 * tile + h], res_ref.at[:, own], (group, tile, h)
                )
            )
        for copy in res_copies:
            copy.start()
        res_ref[:, own] = res_blocks[me]
    flat = jnp.concatenate(
        [jnp.concatenate(residual[half * 8 : half * 8 + 8], axis=1) for half in range(2)], axis=0
    ).astype(BF16)
    back = dot_nt(flat, perm_ref[...])
    for half in range(2):
        for q in range(8):
            rblk_ref[pl.ds(half * PIX + q, 8, stride=8), :] = back[
                half * 8 : half * 8 + 8, q * 128 : q * 128 + 128
            ]
    centre = jnp.concatenate([rblk_ref[0:PIX, :], rblk_ref[PIX : 2 * PIX, :]], axis=1)
    lane = iota((PIX, 256), 1)
    above = jnp.where(lane >= 16, pltpu.roll(centre, 16, 1), 0.0)
    below = jnp.where(lane < 240, pltpu.roll(centre, 240, 1), 0.0)
    stacked = jnp.concatenate([above, centre, below, jnp.zeros((PIX, 256), F32)], axis=0)
    zoned = jnp.concatenate(
        [jnp.where(zone_row == float(z), stacked, 0.0) for z in range(ZONES)], axis=0
    ).astype(BF16)

    for p in range(8):
        grad_ref[p] = dot(table_ref[p * rows : p * rows + rows, :], zoned)
    stores = []
    for half in range(2):
        wide = jnp.concatenate(
            [grad_ref[p, :, half * 128 : half * 128 + 128] for p in range(8)], axis=1
        )
        high = wide.astype(BF16)
        low = (wide - high.astype(F32)).astype(BF16)
        grows_ref[...] = dot(high, perm_ref[...]) + dot(low, perm_ref[...])
        span = slice(half * 64, half * 64 + 64)

        def update(b, carry):
            at = pl.ds(pl.multiple_of(b * 8, 8), 8)
            gradient = jnp.concatenate(
                [grows_ref[at, k * 128 : k * 128 + 128] for k in range(8)], axis=0
            )
            total = gradient + prior_ref[b, span]
            new_ref[b, span] = (cube_ref[b, span].astype(F32) - step_ref[b] * total).astype(BF16)
            return carry

        lax.fori_loop(0, bands, update, 0, unroll=4)
        store = pltpu.make_async_copy(
            new_ref.at[:, span], out_hbm.at[:, span], load_sem.at[3 + half]
        )
        store.start()
        stores.append(store)
    for store in stores:
        store.wait()
    for copy in res_copies:
        copy.wait()


def per_device(
    tiles, cube, kernels, zone_map, kernel_index, measurement, step_size, spectral_weight,
    prior_taps,
):
    bands, height, width = cube.shape
    strip = measurement.shape[0]
    rows = bands * BLOCK
    direct = strip == BLOCK and width == 128
    if direct:
        image = measurement
        sems = 3 + 2 * tiles + tiles
    else:
        moved = lax.all_to_all(measurement, "tile", split_axis=1, concat_axis=0, tiled=True)
        both = lax.all_gather(moved, "band", axis=0, tiled=False)
        image = both.reshape(2, tiles, strip, width).transpose(1, 0, 2, 3).reshape(height, width)
        sems = 4
    hbm = pl.BlockSpec(memory_space=pltpu.HBM)
    vmem = pl.BlockSpec(memory_space=pltpu.VMEM)
    smem = pl.BlockSpec(memory_space=pltpu.SMEM)
    updated, residual = pl.pallas_call(
        functools.partial(kernel, tiles, direct),
        out_shape=(
            jax.ShapeDtypeStruct(cube.shape, BF16),
            jax.ShapeDtypeStruct(image.shape, F32),
        ),
        in_specs=[hbm, hbm, vmem, hbm if direct else vmem] + [smem] * 4,
        out_specs=(hbm, vmem),
        scratch_shapes=[
            pltpu.VMEM(cube.shape, BF16),
            pltpu.VMEM(cube.shape, BF16),
            pltpu.VMEM((rows, 1024), F32),
            pltpu.VMEM((512, 384), BF16),
            pltpu.VMEM((1024, 384), F32),
            pltpu.VMEM(kernels.shape, BF16),
            pltpu.VMEM((height // BLOCK, BLOCK, width), F32),
            pltpu.VMEM((height // BLOCK, BLOCK, width), F32),
            pltpu.VMEM((1024, 1024), BF16),
            pltpu.VMEM((rows, 2048), BF16),
            pltpu.VMEM((256, 8 * rows), BF16),
            pltpu.VMEM((8 * rows, ZONES * 256), BF16),
            pltpu.VMEM((kernels.shape[0], PIX, 256), F32),
            pltpu.VMEM((8, rows, 256), F32),
            pltpu.VMEM(cube.shape, F32),
            pltpu.VMEM((height, width), BF16),
            pltpu.VMEM((rows, 128), BF16),
            pltpu.VMEM((2, rows, 128), BF16),
            pltpu.VMEM((rows, 128), F32),
            pltpu.VMEM((2 * PIX, 128), F32),
            pltpu.VMEM((2 * PIX, 128), F32),
            pltpu.VMEM((2 * PIX, 128), F32),
            pltpu.SemaphoreType.DMA((5,)),
            pltpu.SemaphoreType.DMA((sems,)),
            pltpu.SemaphoreType.DMA((sems,)),
        ],
        compiler_params=pltpu.CompilerParams(
            collective_id=0, has_side_effects=True, vmem_limit_bytes=62 << 20
        ),
    )(cube, kernels, zone_map, image, kernel_index.T, step_size, spectral_weight, prior_taps)
    if direct:
        return updated, residual
    own = lax.dynamic_index_in_dim(
        residual.reshape(tiles, 2, strip, width), lax.axis_index("band"), 1, keepdims=False
    ).reshape(tiles * strip, width)
    return updated, lax.all_to_all(own, "tile", split_axis=0, concat_axis=1, tiled=True)


def solution(mesh):
    return jax.shard_map(
        functools.partial(per_device, mesh.shape["tile"]),
        mesh=mesh,
        in_specs=(
            P(("groups", "band"), None, "tile"),
            P(),
            P(None, "tile"),
            P(),
            P(("groups", "tile", "band"), None),
            P("band"),
            P("band"),
            P(),
        ),
        out_specs=(P(("groups", "band"), None, "tile"), P(("groups", "tile", "band"), None)),
        check_vma=False,
    )
```
